1024 devices in a mesh: rep: 32 (over y, z_hi), fsdp: 32 (over x, z_lo, core).
Axes of the slice: x: 8, y: 8, z: 8 (z_hi: 4, z_lo: 2; z = z_hi * 2 + z_lo), core: 2. Of those that a mesh axis runs over, the one named last changes fastest.
Arguments:
- tokens: bfloat16 [32, 512, 8192], P('rep', None, 'fsdp'), may hold values from -6 to 6
- targets: bfloat16 [32, 512, 1024], P('rep', 'fsdp'), may hold values from -6 to 6
- inner_weights: float32 [32, 8192, 1024], P('rep', 'fsdp'), may hold values from -6 to 6
- outer_weights: float32 [8192, 1024], P('fsdp'), may hold values from -6 to 6
- outer_momentum: float32 [8192, 1024], P('fsdp'), may hold values from -3 to 3
- replica_weights: bfloat16 [32, 8192, 1024], P('rep', 'fsdp'), may hold values from -6 to 6
Outputs:
- new_inner: float32 [32, 8192, 1024], P('rep', 'fsdp')
- new_outer: float32 [8192, 1024], P('fsdp')
- new_moment: float32 [8192, 1024], P('fsdp')
- merged: bfloat16 [32, 8192, 1024], P('rep', 'fsdp')
The draws below stay inside these ranges and needn't reach their ends.
All inputs are finite; a program needn't handle non-finite values.
Results may differ from the reference program's by a relative error of at most 0.005.
Values may be sent and summed in bfloat16 or wider, within the bound.
A program may use at most 32 MiB of HBM per device.

```python
import jax
import jax.numpy as jnp
from jax import lax

D = 8192
KV = 1024
TOK = 512
INNER = 2
REPS = 32


def levels(key, extent, pieces, low, largest):
    level, own = 1.0, jax.random.fold_in(key, 6)
    for position, parts in pieces:
        steps = jnp.exp(jax.random.uniform(jax.random.fold_in(own, position), (parts,), jnp.float32, low / len(pieces), largest / len(pieces)))
        level = level * jnp.repeat(steps, extent[position] // parts).reshape([-1 if axis == position else 1 for axis in range(len(extent))])
    return level


def gaussian(stream_key, shape, deviation, most, cuts=(), held_as=jnp.bfloat16):
    drawn = jax.random.normal(stream_key, shape, jnp.float32) * deviation
    if len(cuts) > 0:
        drawn = levels(stream_key, shape, cuts, -0.22, 0.18) * drawn
    return jnp.clip(drawn, min=-most, max=most).astype(held_as)


def setup_inputs(seed: int = 0) -> dict:
    seeds = jax.random.split(jax.random.key(seed), 7)
    tokens = gaussian(seeds[0], (REPS, TOK, D), 1.0, 6.0, ((0, 32), (2, 32)))
    targets = gaussian(seeds[1], (REPS, TOK, KV), 1.0, 6.0, ((0, 32), (1, 32)))
    inner_weights = gaussian(seeds[2], (REPS, D, KV), 1.0, 6.0, ((0, 32), (1, 32)), jnp.float32)
    outer_weights = gaussian(seeds[3], (D, KV), 1.0, 6.0, ((0, 32),), jnp.float32)
    outer_momentum = gaussian(seeds[4], (D, KV), 0.5, 3.0, ((0, 32),), jnp.float32)
    replica_weights = gaussian(seeds[5], (REPS, D, KV), 1.0, 6.0, ((0, 32), (1, 32)))
    return {"tokens": tokens, "targets": targets, "inner_weights": inner_weights, "outer_weights": outer_weights, "outer_momentum": outer_momentum, "replica_weights": replica_weights}


inner_rate = 0.5
momentum_coef = 0.9
outer_rate = 0.7
merge_keep = 0.5


def inner_steps(operands):
    token_rows, target_rows, weights_now = operands
    weight_scale = D ** -0.5
    for inner_turn in range(INNER):
        weights_half = weights_now.astype(jnp.bfloat16)
        predicted = jnp.dot(token_rows, weights_half, preferred_element_type=jnp.float32) * weight_scale
        errors = (predicted - target_rows.astype(jnp.float32)).astype(jnp.bfloat16)
        gradient = jnp.dot(token_rows.T, errors, preferred_element_type=jnp.float32) * weight_scale
        weights_now = weights_now - inner_rate * gradient
    return weights_now


def reference(tokens, targets, inner_weights, outer_weights, outer_momentum, replica_weights):
    new_inner = lax.map(inner_steps, (tokens, targets, inner_weights))

    def accumulate(carry, replica_rows):
        return carry + (outer_weights - replica_rows.astype(jnp.float32)), None

    pseudo_sum, unused = lax.scan(accumulate, jnp.zeros_like(outer_weights), replica_weights)
    outer_delta = pseudo_sum / REPS
    new_moment = momentum_coef * outer_momentum + outer_delta
    new_outer = outer_weights - outer_rate * (outer_delta + momentum_coef * new_moment)

    def merge_one(replica_rows):
        mixed = merge_keep * replica_rows.astype(jnp.float32) + (1.0 - merge_keep) * new_outer
        return mixed.astype(jnp.bfloat16)

    merged = lax.map(merge_one, replica_weights)
    return new_inner, new_outer, new_moment, merged
```

```python
import functools

import jax
import jax.numpy as jnp
from jax import lax
from jax.experimental import pallas as pl
from jax.experimental.pallas import tpu as pltpu
from jax.sharding import PartitionSpec as P

D = 8192
REPS = 32
inner_rate = 0.5
momentum_coef = 0.9
outer_rate = 0.7
merge_keep = 0.5

NX, NZ, NC = 8, 2, 2
NY, NH = 8, 4
MESH = pl.DeviceIdType.MESH
F32, BF16 = jnp.float32, jnp.bfloat16


class Copies:
    def __init__(self, send_sems, recv_sems):
        self.send_sems, self.recv_sems = send_sems, recv_sems
        self.made = {}

    def start(self, name, src, dst, device):
        slot = len(self.made)
        assert slot < self.send_sems.shape[0]
        copy = pltpu.make_async_remote_copy(
            src_ref=src,
            dst_ref=dst,
            send_sem=self.send_sems.at[slot],
            recv_sem=self.recv_sems.at[slot],
            device_id=device,
            device_id_type=MESH,
        )
        copy.start()
        self.made[name] = copy

    def arrived(self, name):
        self.made[name].wait_recv()

    def drain(self):
        for copy in self.made.values():
            copy.wait_send()


def hops(direction, block):
    return 4 if (direction == 0) == (block == 0) else 3


def comm_kernel(inner, outer, weight_scale, x_hbm, w_hbm, t_hbm, o_hbm, r_hbm,
                e_out, k_out, d_out,
                xv, wv, tv, ov, rv, qown, qoth, qpar, rx, sx, zs, zr, ek,
                ry, sy, ysum, hr, dv,
                load_sems, store_sems, send_sems, recv_sems):
    rep, fsdp = lax.axis_index("rep"), lax.axis_index("fsdp")
    x, z, c = fsdp // 4, (fsdp // 2) % 2, fsdp % 2
    y, h = rep // 4, rep % 4
    cols = w_hbm.shape[1]
    toks = k_out.shape[-1]
    wide = cols + toks
    half = ov.shape[2] // 2
    quarter = ov.shape[2] // 4

    def at_x(k):
        return lax.rem(x + k + NX, NX)

    def at_y(k):
        return lax.rem(y + k + NY, NY)

    def to_x(k):
        return {"fsdp": at_x(k) * 4 + z * 2 + c}

    def to_y(k):
        return {"rep": at_y(k) * 4 + h}

    def to_h(k):
        return {"rep": y * 4 + lax.rem(h + k, NH)}

    core = {"fsdp": x * 4 + z * 2 + 1 - c}
    zlo = {"fsdp": x * 4 + (1 - z) * 2 + c}

    loads = {}
    for slot, (name, src, dst) in enumerate((("x", x_hbm, xv), ("w", w_hbm, wv), ("o", o_hbm, ov), ("r", r_hbm, rv), ("t", t_hbm, tv))):
        loads[name] = pltpu.make_async_copy(src, dst, load_sems.at[slot])
        loads[name].start()

    barrier = pltpu.get_barrier_semaphore()
    peers = []
    if inner:
        peers += [core, zlo, to_x(1), to_x(-1)]
    if outer:
        peers += [to_y(1), to_y(-1), to_h(1), to_h(2), to_h(3)]
    for peer in peers:
        pl.semaphore_signal(barrier, inc=1, device_id=peer, device_id_type=MESH)

    net = Copies(send_sems, recv_sems)

    def rows_of(core_index):
        return xv[:, :, core_index].reshape(NX * NZ * 16, xv.shape[-1])

    def partial(rows, start, width):
        if start < cols:
            out = jnp.dot(rows, wv[:, start:start + width].astype(BF16), preferred_element_type=F32)
        else:
            every = xv[...].reshape(toks, xv.shape[-1])
            out = lax.dot_general(rows, every, (((1,), (1,)), ((), ())), preferred_element_type=F32)
        return out.reshape(NX, NZ, 16, width)

    tiles = [(start, cols // 2) for start in (0, cols // 2)] + [(cols, toks)]

    loads["x"].wait()
    loads["w"].wait()
    if inner:
        rows = rows_of(1 - c)
        for start, width in tiles:
            qoth[:, :, :, start:start + width] = partial(rows, start, width).astype(BF16)

    pl.semaphore_wait(barrier, len(peers))

    if inner:
        for k in (4, 3, 5, 2, 6, 1, 7, 0):
            net.start(("core", k), qoth.at[at_x(k)], qpar.at[at_x(k)], core)

    def y_own(k, block):
        at = slice(block * half, (block + 1) * half)
        return ov[at_y(k), :, at] - rv[at_y(k), :, at].astype(F32)

    def y_send(direction, block, j):
        step = 1 if direction == 0 else -1
        value = y_own(step * j, block)
        if j < hops(direction, block):
            net.arrived(("ry", direction, block, j + 1))
            value = value + ry[direction, block, j].astype(F32)
        sy[direction, block, j - 1] = value.astype(BF16)
        net.start(("ry", direction, block, j), sy.at[direction, block, j - 1], ry.at[direction, block, j - 1], to_y(step))

    def y_final(block):
        for direction in (0, 1):
            net.arrived(("ry", direction, block, 1))
        at = slice(block * half, (block + 1) * half)
        ysum[:, at] = y_own(0, block) + (ry[0, block, 0].astype(F32) + ry[1, block, 0].astype(F32))

    merged = set()

    def merge(k):
        k = k % NX
        if k not in merged:
            merged.add(k)
            net.arrived(("core", k))
            qown[at_x(k)] = qown[at_x(k)] + qpar[at_x(k)].astype(F32)

    def zz(block):
        return 1 - z if block == 0 else z

    def x_send(direction, block, j):
        step = 1 if direction == 0 else -1
        merge(step * j)
        value = qown[at_x(step * j), zz(block)]
        if j < hops(direction, block):
            net.arrived(("rx", direction, block, j + 1))
            value = value + rx[direction, block, j].astype(F32)
        sx[direction, block, j - 1] = value.astype(BF16)
        net.start(("rx", direction, block, j), sx.at[direction, block, j - 1], rx.at[direction, block, j - 1], to_x(step))

    def x_final(block):
        merge(0)
        for direction in (0, 1):
            net.arrived(("rx", direction, block, 1))
        return qown[x, zz(block)] + (rx[0, block, 0].astype(F32) + rx[1, block, 0].astype(F32))

    order = ((0, 0), (1, 1), (0, 1), (1, 0))

    if outer:
        loads["o"].wait()
        loads["r"].wait()
        for direction, block in order:
            y_send(direction, block, hops(direction, block))
    if inner:
        rows = rows_of(c)
        for start, width in tiles:
            qown[:, :, :, start:start + width] = partial(rows, start, width)
        for direction, block in order:
            x_send(direction, block, hops(direction, block))
    for j in (3, 2, 1):
        for ring, send in ((outer, y_send), (inner, x_send)):
            if ring:
                for direction, block in order:
                    if j < hops(direction, block):
                        send(direction, block, j)

    if outer:
        y_final(0)
        y_final(1)
        for k in (2, 1, 3):
            at = pl.ds(pl.multiple_of(lax.rem(h + k, NH) * quarter, 128), quarter)
            net.start(("hr", k), ysum.at[:, at], hr.at[k - 1], to_h(k))
    if inner:
        zs[...] = x_final(0).astype(BF16)
        net.start("zr", zs, zr, zlo)
        mine = x_final(1)
        loads["t"].wait()
        net.arrived("zr")
        total = mine + zr[...].astype(F32)
        ek[x, z, c, :, 0:cols] = (total[:, 0:cols] * weight_scale - tv[...].astype(F32)).astype(BF16)
        ek[x, z, c, :, cols:wide] = total[:, cols:wide].astype(BF16)

    def g_slot(k, block):
        return ek.at[at_x(k), z if block == 0 else 1 - z, c]

    def g_pass(direction, block, i):
        step = 1 if direction == 0 else -1
        slot = g_slot(-step * i, block)
        if i > 0:
            net.arrived(("gx", direction, block, i))
            net.start(("gc", direction, block, i), slot, slot, core)
        if i < hops(direction, block):
            net.start(("gx", direction, block, i + 1), slot, slot, to_x(step))

    def g_own(block):
        slot = g_slot(0, block)
        for direction in (0, 1):
            g_pass(direction, block, 0)
        net.start(("gc", block), slot, slot, core)

    def d_slot(k, block):
        return dv.at[at_y(k), :, block * half:(block + 1) * half]

    def d_pass(direction, block, i):
        step = 1 if direction == 0 else -1
        slot = d_slot(-step * i, block)
        if i > 0:
            net.arrived(("gy", direction, block, i))
        if i < hops(direction, block):
            net.start(("gy", direction, block, i + 1), slot, slot, to_y(step))

    def g_hop(block, i):
        if inner:
            for direction in (0, 1):
                if i <= hops(direction, block):
                    g_pass(direction, block, i)

    def d_hop(i):
        if outer:
            for direction, block in order:
                if i <= hops(direction, block):
                    d_pass(direction, block, i)

    if inner:
        slot = g_slot(0, 0)
        net.start("gz", slot, slot, zlo)
        g_own(0)
    if outer:
        own = pl.ds(pl.multiple_of(h * quarter, 128), quarter)
        value = ysum[:, own]
        for k in (1, 3, 2):
            net.arrived(("hr", k))
            value = value + hr[k - 1]
        dv[y, :, own] = value / REPS
        for k in (2, 1, 3):
            net.start(("gh", k), dv.at[y, :, own], dv.at[y, :, own], to_h(k))
    g_hop(0, 1)
    if inner:
        net.arrived("gz")
        g_own(1)
    g_hop(0, 2)
    g_hop(1, 1)
    if outer:
        for k in (1, 3, 2):
            net.arrived(("gh", k))
    d_hop(0)
    g_hop(0, 3)
    g_hop(1, 2)
    d_hop(1)
    g_hop(0, 4)
    g_hop(1, 3)
    d_hop(2)
    g_hop(1, 4)
    d_hop(3)
    if inner:
        for name in list(net.made):
            if name[0] == "gc":
                net.arrived(name)
    stores = []
    if inner:
        stores.append(pltpu.make_async_copy(ek.at[:, :, :, :, 0:cols], e_out, store_sems.at[0]))
        stores.append(pltpu.make_async_copy(ek.at[:, :, :, :, cols:wide], k_out, store_sems.at[1]))
        for store in stores:
            store.start()
    d_hop(4)
    if outer:
        stores.append(pltpu.make_async_copy(dv, d_out, store_sems.at[2]))
        stores[-1].start()
    for store in stores:
        store.wait()
    if not inner:
        loads["t"].wait()
    if not outer:
        loads["o"].wait()
        loads["r"].wait()
    net.drain()


def exchange(tokens, targets, weights, outer_weights, replica, inner=True, outer=True):
    toks, feats = tokens.shape
    cols = weights.shape[1]
    wide = cols + toks
    o_cols = outer_weights.shape[1]
    y_rows = outer_weights.shape[0] // NY
    weight_scale = D ** (-0.5)
    hbm = pl.BlockSpec(memory_space=pl.ANY)
    copies = 88
    e, k, delta = pl.pallas_call(
        functools.partial(comm_kernel, inner, outer, weight_scale),
        out_shape=(
            jax.ShapeDtypeStruct((NX, NZ, NC, 16, cols), BF16),
            jax.ShapeDtypeStruct((NX, NZ, NC, 16, toks), BF16),
            jax.ShapeDtypeStruct((NY, y_rows, o_cols), F32),
        ),
        in_specs=[hbm] * 5,
        out_specs=(hbm,) * 3,
        scratch_shapes=[
            pltpu.VMEM((NX, NZ, NC, 16, feats), BF16),
            pltpu.VMEM((feats, cols), F32),
            pltpu.VMEM((16, cols), BF16),
            pltpu.VMEM((NY, y_rows, o_cols), F32),
            pltpu.VMEM((NY, y_rows, o_cols), BF16),
            pltpu.VMEM((NX, NZ, 16, wide), F32),
            pltpu.VMEM((NX, NZ, 16, wide), BF16),
            pltpu.VMEM((NX, NZ, 16, wide), BF16),
            pltpu.VMEM((2, 2, 4, 16, wide), BF16),
            pltpu.VMEM((2, 2, 4, 16, wide), BF16),
            pltpu.VMEM((16, wide), BF16),
            pltpu.VMEM((16, wide), BF16),
            pltpu.VMEM((NX, NZ, NC, 16, wide), BF16),
            pltpu.VMEM((2, 2, 4, y_rows, o_cols // 2), BF16),
            pltpu.VMEM((2, 2, 4, y_rows, o_cols // 2), BF16),
            pltpu.VMEM((y_rows, o_cols), F32),
            pltpu.VMEM((3, y_rows, o_cols // 4), F32),
            pltpu.VMEM((NY, y_rows, o_cols), F32),
            pltpu.SemaphoreType.DMA((5,)),
            pltpu.SemaphoreType.DMA((3,)),
            pltpu.SemaphoreType.DMA((copies,)),
            pltpu.SemaphoreType.DMA((copies,)),
        ],
        compiler_params=pltpu.CompilerParams(collective_id=0, has_side_effects=True),
    )(
        tokens.reshape(NX, NZ, NC, 16, feats),
        weights,
        targets,
        outer_weights.reshape(NY, y_rows, o_cols),
        replica.reshape(NY, y_rows, o_cols),
    )
    return e.reshape(toks, cols), k.reshape(toks, toks), delta.reshape(outer_weights.shape)


def local(tokens, targets, inner_weights, outer_weights, outer_momentum, replica_weights):
    token_cols, replica = tokens[0], replica_weights[0]
    errors, products, outer_delta = exchange(token_cols, targets[0], inner_weights[0], outer_weights, replica)

    new_moment = momentum_coef * outer_momentum + outer_delta
    new_outer = outer_weights - outer_rate * (outer_delta + momentum_coef * new_moment)
    mixed = merge_keep * replica.astype(F32) + (1.0 - merge_keep) * new_outer

    turned = jnp.dot(products, token_cols, preferred_element_type=F32)
    both = (2.0 * token_cols.astype(F32) - (inner_rate / D) * turned).astype(BF16)
    gradient = lax.dot_general(both, errors, (((0,), (0,)), ((), ())), preferred_element_type=F32)
    new_inner = inner_weights[0] - (inner_rate * D ** (-0.5)) * gradient
    return (new_inner[None], new_outer, new_moment, mixed.astype(BF16)[None])


def solution(mesh):
    placed = (
        P("rep", None, "fsdp"),
        P("rep", "fsdp", None),
        P("rep", "fsdp", None),
        P("fsdp", None),
        P("fsdp", None),
        P("rep", "fsdp", None),
    )
    return jax.shard_map(
        local,
        mesh=mesh,
        in_specs=placed,
        out_specs=(
            P("rep", "fsdp", None),
            P("fsdp", None),
            P("fsdp", None),
            P("rep", "fsdp", None),
        ),
        check_vma=False,
    )
```

```python
import functools

import jax
import jax.numpy as jnp
from jax import lax
from jax.experimental import pallas as pl
from jax.experimental.pallas import tpu as pltpu
from jax.sharding import PartitionSpec as P

D = 8192
REPS = 32
inner_rate = 0.5
momentum_coef = 0.9
outer_rate = 0.7
merge_keep = 0.5

NX, NZ, NC = 8, 2, 2
NY, NH = 8, 4
MESH = pl.DeviceIdType.MESH
F32, BF16 = jnp.float32, jnp.bfloat16


class Copies:
    def __init__(self, send_sems, recv_sems):
        self.send_sems, self.recv_sems = send_sems, recv_sems
        self.made, self.guards, self.slots = {}, {}, 0

    def make(self, name, src, dst, device, recv_like=None, guard=None):
        slot = self.slots
        self.slots += 1
        assert slot < self.send_sems.shape[0]
        recv_slot = slot if recv_like is None else self.made[recv_like][1]
        copy = pltpu.make_async_remote_copy(
            src_ref=src,
            dst_ref=dst,
            send_sem=self.send_sems.at[slot],
            recv_sem=self.recv_sems.at[recv_slot],
            device_id=device,
            device_id_type=MESH,
        )
        self.made[name] = (copy, recv_slot, guard)
        return copy

    def start(self, name, src, dst, device):
        self.make(name, src, dst, device).start()

    def begin(self, name):
        self.made[name][0].start()

    def arrived(self, name):
        self.made[name][0].wait_recv()

    def drain(self):
        for copy, _, guard in self.made.values():
            if guard is None:
                copy.wait_send()
            else:
                pl.when(guard)(copy.wait_send)


def enc(value):
    return (value * jnp.abs(value) * (value * value)).astype(BF16)


def dec(coded):
    coded = coded.astype(F32)
    root = jnp.sqrt(jnp.sqrt(jnp.abs(coded)))
    return jnp.where(coded < 0.0, -root, root)


YB = 4


def hops(direction, block, blocks):
    return 4 if (direction == 0) == (block < blocks // 2) else 3


def comm_kernel(inner, outer, weight_scale, x_hbm, w_hbm, t_hbm, o_hbm, r_hbm, m_hbm,
                w_out, o_out, m_out, r_out,
                xv, xt, wv, tv, ov, rv, mv, qown, qoth, qpar, rx, sx, zs, zr, ek,
                ry, sy, ysum, us, ub, dv,
                load_sems, send_sems, recv_sems):
    rep, fsdp = lax.axis_index("rep"), lax.axis_index("fsdp")
    x, z, c = fsdp // 4, (fsdp // 2) % 2, fsdp % 2
    y, h = rep // 4, rep % 4
    feats, cols = wv.shape
    toks = xt.shape[1]
    wide = cols + toks
    ycols = ov.shape[2] // YB

    def at_x(k):
        return lax.rem(x + k + NX, NX)

    def at_y(k):
        return lax.rem(y + k + NY, NY)

    def to_x(k):
        return {"fsdp": at_x(k) * 4 + z * 2 + c}

    def to_y(k):
        return {"rep": at_y(k) * 4 + h}

    def to_h(at):
        return {"rep": y * 4 + at}

    core = {"fsdp": x * 4 + z * 2 + 1 - c}
    zlo = {"fsdp": x * 4 + (1 - z) * 2 + c}
    above, below = lax.rem(h + 1, NH), lax.rem(h + NH - 1, NH)
    first, last = h == 0, h == NH - 1

    loads = {}
    for slot, (name, src, dst) in enumerate((("o", o_hbm, ov), ("r", r_hbm, rv), ("x", x_hbm, xv), ("w", w_hbm, wv), ("t", t_hbm, tv), ("m", m_hbm, mv))):
        loads[name] = pltpu.make_async_copy(src, dst, load_sems.at[slot])
        loads[name].start()

    barrier = pltpu.get_barrier_semaphore()

    def greet(peer):
        pl.semaphore_signal(barrier, inc=1, device_id=peer, device_id_type=MESH)

    expected = 0
    if inner:
        for peer in (core, zlo, to_x(1), to_x(-1)):
            greet(peer)
        expected += 4
    if outer:
        greet(to_y(1))
        greet(to_y(-1))

        @pl.when(jnp.logical_not(last))
        def _():
            greet(to_h(above))

        @pl.when(jnp.logical_not(first))
        def _():
            greet(to_h(below))

        expected += 2 + jnp.where(last, 0, 1) + jnp.where(first, 0, 1)

    net = Copies(send_sems, recv_sems)

    def ycut(block):
        return slice(block * ycols, (block + 1) * ycols)

    def y_own(k, block):
        return ov[at_y(k), :, ycut(block)] - rv[at_y(k), :, ycut(block)].astype(F32)

    def y_send(direction, block, j):
        step = 1 if direction == 0 else -1
        value = y_own(step * j, block)
        if j < hops(direction, block, YB):
            net.arrived(("ry", direction, block, j + 1))
            value = value + dec(ry[direction, block, j])
        sy[direction, block, j - 1] = enc(value)
        net.start(("ry", direction, block, j), sy.at[direction, block, j - 1], ry.at[direction, block, j - 1], to_y(step))

    y_order = ((0, 0), (1, 2), (0, 1), (1, 3), (0, 2), (1, 0), (0, 3), (1, 1))

    def y_first():
        for direction, block in y_order:
            y_send(direction, block, hops(direction, block, YB))

    def y_round(j):
        if outer:
            for direction, block in y_order:
                if j < hops(direction, block, YB):
                    y_send(direction, block, j)

    def y_final(block):
        for direction in (0, 1):
            net.arrived(("ry", direction, block, 1))
        at = ycut(block)
        ysum[:, at] = y_own(0, block) + (dec(ry[0, block, 0]) + dec(ry[1, block, 0]))
        net.make(("up", block), us.at[:, at], ub.at[:, at], to_h(above), guard=jnp.logical_not(last))
        slot = dv.at[y, :, at]
        for target in range(NH - 1):
            net.make(("down", block, target), slot, slot, to_h(target), recv_like=("down", block, 0) if target else None, guard=last)

        @pl.when(jnp.logical_not(first))
        def _():
            net.arrived(("up", block))
            ysum[:, at] = ysum[:, at] + dec(ub[:, at])

        @pl.when(jnp.logical_not(last))
        def _():
            us[:, at] = enc(ysum[:, at])
            net.begin(("up", block))

        @pl.when(last)
        def _():
            dv[y, :, at] = enc(ysum[:, at] / REPS)
            for target in range(NH - 1):
                net.begin(("down", block, target))

    def rows_of(core_index):
        return xv[:, :, core_index].reshape(NX * NZ * 16, feats)

    def partial(rows, start, width):
        if start < cols:
            right = wv[:, start:start + width].astype(BF16)
        else:
            right = xt[...]
        return jnp.dot(rows, right, preferred_element_type=F32).reshape(NX, NZ, 16, width)

    tiles = [(start, cols // 2) for start in (0, cols // 2)] + [(cols, toks)]

    merged = set()

    def merge(k):
        k = k % NX
        if k not in merged:
            merged.add(k)
            net.arrived(("core", k))
            qown[at_x(k)] = qown[at_x(k)] + qpar[at_x(k)].astype(F32)

    def zz(block):
        return 1 - z if block == 0 else z

    def x_send(direction, block, j):
        step = 1 if direction == 0 else -1
        merge(step * j)
        value = qown[at_x(step * j), zz(block)]
        if j < hops(direction, block, 2):
            net.arrived(("rx", direction, block, j + 1))
            value = value + rx[direction, block, j].astype(F32)
        sx[direction, block, j - 1] = value.astype(BF16)
        net.start(("rx", direction, block, j), sx.at[direction, block, j - 1], rx.at[direction, block, j - 1], to_x(step))

    def x_final(block):
        merge(0)
        for direction in (0, 1):
            net.arrived(("rx", direction, block, 1))
        return qown[x, zz(block)] + (rx[0, block, 0].astype(F32) + rx[1, block, 0].astype(F32))

    x_order = ((0, 0), (1, 1), (0, 1), (1, 0))

    def x_round(j):
        if inner:
            for direction, block in x_order:
                if j < hops(direction, block, 2):
                    x_send(direction, block, j)

    def g_slot(k, block):
        return ek.at[at_x(k), z if block == 0 else 1 - z, c]

    def g_pass(direction, block, i):
        step = 1 if direction == 0 else -1
        slot = g_slot(-step * i, block)
        if i > 0:
            net.arrived(("gx", direction, block, i))
        if i < hops(direction, block, 2):
            net.start(("gx", direction, block, i + 1), slot, slot, to_x(step))
        if i > 0:
            net.start(("gc", direction, block, i), slot, slot, core)

    def g_own(block):
        slot = g_slot(0, block)
        for direction in (0, 1):
            g_pass(direction, block, 0)
        net.start(("gc", block), slot, slot, core)

    def g_hop(block, i):
        if inner:
            for direction in (0, 1):
                if i <= hops(direction, block, 2):
                    g_pass(direction, block, i)

    def d_pass(direction, block, i):
        step = 1 if direction == 0 else -1
        slot = dv.at[at_y(-step * i), :, ycut(block)]
        if i > 0:
            net.arrived(("gy", direction, block, i))
        if i < hops(direction, block, YB):
            net.start(("gy", direction, block, i + 1), slot, slot, to_y(step))

    def d_own(block):
        @pl.when(jnp.logical_not(last))
        def _():
            net.arrived(("down", block, 0))

        for direction in (0, 1):
            d_pass(direction, block, 0)

    def d_finish(k, block):
        at, row = ycut(block), at_y(k)
        delta = dec(dv[row, :, at])
        moment = momentum_coef * mv[row, :, at] + delta
        moved = ov[row, :, at] - outer_rate * (delta + momentum_coef * moment)
        m_out[row, :, at] = moment
        o_out[row, :, at] = moved
        r_out[row, :, at] = (merge_keep * rv[row, :, at].astype(F32) + (1.0 - merge_keep) * moved).astype(BF16)

    def d_hop(i):
        if outer:
            pieces = [piece for piece in y_order if i <= hops(*piece, YB)]
            for direction, block in pieces:
                d_pass(direction, block, i)
            for direction, block in pieces:
                d_finish(-i if direction == 0 else i, block)

    if outer:
        loads["o"].wait()
        loads["r"].wait()
    pl.semaphore_wait(barrier, expected)
    if outer:
        y_first()
    loads["x"].wait()
    loads["w"].wait()
    if inner:
        xt[...] = xv[...].reshape(toks, feats).T
        rows = rows_of(1 - c)
        for start, width in tiles:
            qoth[:, :, :, start:start + width] = partial(rows, start, width).astype(BF16)
        for k in (4, 3, 5, 2, 6, 1, 7, 0):
            net.start(("core", k), qoth.at[at_x(k)], qpar.at[at_x(k)], core)
    y_round(3)
    if inner:
        rows = rows_of(c)
        for start, width in tiles:
            qown[:, :, :, start:start + width] = partial(rows, start, width)
        for direction, block in x_order:
            x_send(direction, block, hops(direction, block, 2))
    y_round(2)
    x_round(3)
    y_round(1)
    x_round(2)
    if outer:
        for block in (0, 2, 1, 3):
            y_final(block)
    x_round(1)
    if inner:
        zs[...] = x_final(0).astype(BF16)
        net.start("zr", zs, zr, zlo)
        mine = x_final(1)
        loads["t"].wait()
        net.arrived("zr")
        total = mine + zr[...].astype(F32)
        ek[x, z, c, :, 0:cols] = (total[:, 0:cols] * weight_scale - tv[...].astype(F32)).astype(BF16)
        ek[x, z, c, :, cols:wide] = total[:, cols:wide].astype(BF16)
        slot = g_slot(0, 0)
        net.start("gz", slot, slot, zlo)
        g_own(0)
    g_hop(0, 1)
    if inner:
        net.arrived("gz")
        g_own(1)
    g_hop(0, 2)
    g_hop(1, 1)
    g_hop(0, 3)
    g_hop(1, 2)
    g_hop(0, 4)
    g_hop(1, 3)
    if outer:
        for block in (0, 2, 1, 3):
            d_own(block)
    g_hop(1, 4)
    if outer:
        loads["m"].wait()
        for block in range(YB):
            d_finish(0, block)
    d_hop(1)
    if inner:
        for name in list(net.made):
            if name[0] == "gc":
                net.arrived(name)
        turned = jnp.dot(xt[...], ek[:, :, :, :, cols:wide].reshape(toks, toks), preferred_element_type=F32)
        both = (2.0 * xt[...].astype(F32) - (inner_rate / D) * turned).astype(BF16)
    d_hop(2)
    if inner:
        for start in range(0, cols, cols // 2):
            at = slice(start, start + cols // 2)
            gradient = jnp.dot(both, ek[:, :, :, :, at].reshape(toks, cols // 2), preferred_element_type=F32)
            w_out[:, at] = wv[:, at] - (inner_rate * weight_scale) * gradient
    d_hop(3)
    d_hop(4)
    if not inner:
        loads["t"].wait()
    if not outer:
        loads["o"].wait()
        loads["r"].wait()
        loads["m"].wait()
    net.drain()


def exchange(tokens, targets, weights, outer_weights, moment, replica, inner=True, outer=True):
    toks, feats = tokens.shape
    cols = weights.shape[1]
    wide = cols + toks
    o_cols = outer_weights.shape[1]
    y_rows = outer_weights.shape[0] // NY
    weight_scale = D ** (-0.5)
    hbm = pl.BlockSpec(memory_space=pl.ANY)
    copies = 140
    results = pl.pallas_call(
        functools.partial(comm_kernel, inner, outer, weight_scale),
        out_shape=(
            jax.ShapeDtypeStruct((feats, cols), F32),
            jax.ShapeDtypeStruct((NY, y_rows, o_cols), F32),
            jax.ShapeDtypeStruct((NY, y_rows, o_cols), F32),
            jax.ShapeDtypeStruct((NY, y_rows, o_cols), BF16),
        ),
        in_specs=[hbm] * 6,
        out_specs=(pl.BlockSpec(memory_space=pltpu.VMEM),) * 4,
        scratch_shapes=[
            pltpu.VMEM((NX, NZ, NC, 16, feats), BF16),
            pltpu.VMEM((feats, toks), BF16),
            pltpu.VMEM((feats, cols), F32),
            pltpu.VMEM((16, cols), BF16),
            pltpu.VMEM((NY, y_rows, o_cols), F32),
            pltpu.VMEM((NY, y_rows, o_cols), BF16),
            pltpu.VMEM((NY, y_rows, o_cols), F32),
            pltpu.VMEM((NX, NZ, 16, wide), F32),
            pltpu.VMEM((NX, NZ, 16, wide), BF16),
            pltpu.VMEM((NX, NZ, 16, wide), BF16),
            pltpu.VMEM((2, 2, 4, 16, wide), BF16),
            pltpu.VMEM((2, 2, 4, 16, wide), BF16),
            pltpu.VMEM((16, wide), BF16),
            pltpu.VMEM((16, wide), BF16),
            pltpu.VMEM((NX, NZ, NC, 16, wide), BF16),
            pltpu.VMEM((2, YB, 4, y_rows, o_cols // YB), BF16),
            pltpu.VMEM((2, YB, 4, y_rows, o_cols // YB), BF16),
            pltpu.VMEM((y_rows, o_cols), F32),
            pltpu.VMEM((y_rows, o_cols), BF16),
            pltpu.VMEM((y_rows, o_cols), BF16),
            pltpu.VMEM((NY, y_rows, o_cols), BF16),
            pltpu.SemaphoreType.DMA((6,)),
            pltpu.SemaphoreType.DMA((copies,)),
            pltpu.SemaphoreType.DMA((copies,)),
        ],
        compiler_params=pltpu.CompilerParams(collective_id=0, has_side_effects=True, vmem_limit_bytes=32 << 20),
    )(
        *(pltpu.with_memory_space_constraint(array, pltpu.HBM) for array in (
            tokens.reshape(NX, NZ, NC, 16, feats),
            weights,
            targets,
            outer_weights.reshape(NY, y_rows, o_cols),
            replica.reshape(NY, y_rows, o_cols),
            moment.reshape(NY, y_rows, o_cols),
        ))
    )
    return results[0], *(result.reshape(outer_weights.shape) for result in results[1:])


def local(tokens, targets, inner_weights, outer_weights, outer_momentum, replica_weights):
    new_inner, new_outer, new_moment, merged = exchange(
        tokens[0], targets[0], inner_weights[0], outer_weights, outer_momentum, replica_weights[0]
    )
    return (new_inner[None], new_outer, new_moment, merged[None])


def solution(mesh):
    placed = (
        P("rep", None, "fsdp"),
        P("rep", "fsdp", None),
        P("rep", "fsdp", None),
        P("fsdp", None),
        P("fsdp", None),
        P("rep", "fsdp", None),
    )
    return jax.shard_map(
        local,
        mesh=mesh,
        in_specs=placed,
        out_specs=(
            P("rep", "fsdp", None),
            P("fsdp", None),
            P("fsdp", None),
            P("rep", "fsdp", None),
        ),
        check_vma=False,
    )
```

```python
import functools

import jax
import jax.numpy as jnp
from jax import lax
from jax.experimental import pallas as pl
from jax.experimental.pallas import tpu as pltpu
from jax.sharding import PartitionSpec as P

D = 8192
REPS = 32
inner_rate = 0.5
momentum_coef = 0.9
outer_rate = 0.7
merge_keep = 0.5

NX, NZ, NC = 8, 2, 2
NY, NH = 8, 4
MESH = pl.DeviceIdType.MESH
F32, BF16 = jnp.float32, jnp.bfloat16


class Copies:
    def __init__(self, send_sems, recv_sems, slots=None, made=None):
        self.send_sems, self.recv_sems = send_sems, recv_sems
        self.slots = {} if slots is None else slots
        self.made = {} if made is None else dict(made)

    def branch(self):
        return Copies(self.send_sems, self.recv_sems, self.slots, self.made)

    def make(self, name, src, dst, device, recv_like=None, guard=None):
        slot = self.slots.setdefault(name, len(self.slots))
        assert slot < self.send_sems.shape[0]
        copy = pltpu.make_async_remote_copy(
            src_ref=src,
            dst_ref=dst,
            send_sem=self.send_sems.at[slot],
            recv_sem=self.recv_sems.at[slot if recv_like is None else self.slots[recv_like]],
            device_id=device,
            device_id_type=MESH,
        )
        self.made[name] = (copy, guard)
        return copy

    def start(self, name, src, dst, device):
        self.make(name, src, dst, device).start()

    def begin(self, name):
        self.made[name][0].start()

    def arrived(self, name):
        self.made[name][0].wait_recv()

    def drain(self):
        for copy, guard in self.made.values():
            if guard is None:
                copy.wait_send()
            else:
                pl.when(guard)(copy.wait_send)


def enc(value):
    return (value * jnp.abs(value) * (value * value)).astype(BF16)


def dec(coded):
    coded = coded.astype(F32)
    root = jnp.sqrt(jnp.sqrt(jnp.abs(coded)))
    return jnp.where(coded < 0.0, -root, root)


YB = 4
XH = 2
XB = 2 * XH


def hops(direction, block, blocks):
    return 4 if (direction == 0) == (block < blocks // 2) else 3


def comm_kernel(inner, outer, weight_scale, x_hbm, w_hbm, t_hbm, o_hbm, r_hbm, m_hbm,
                w_out, o_out, m_out, r_out,
                xv, xt, wv, wb, tv, ov, rv, mv, qown, qoth, qpar, rx, sx, zs, zr, ek,
                ry, sy, ysum, us, ub, dv,
                load_sems, send_sems, recv_sems):
    rep, fsdp = lax.axis_index("rep"), lax.axis_index("fsdp")
    x, z, c = fsdp // 4, (fsdp // 2) % 2, fsdp % 2
    y, h = rep // 4, rep % 4
    feats, cols = wv.shape
    toks = xt.shape[1]
    wide = cols + toks
    ycols = ov.shape[2] // YB

    def at_x(k):
        return lax.rem(x + k + NX, NX)

    def at_y(k):
        return lax.rem(y + k + NY, NY)

    def to_x(k):
        return {"fsdp": at_x(k) * 4 + z * 2 + c}

    def to_y(k):
        return {"rep": at_y(k) * 4 + h}

    def to_h(at):
        return {"rep": y * 4 + at}

    core = {"fsdp": x * 4 + z * 2 + 1 - c}
    zlo = {"fsdp": x * 4 + (1 - z) * 2 + c}
    above, below = lax.rem(h + 1, NH), lax.rem(h + NH - 1, NH)
    first, last = h == 0, h == NH - 1

    loads = {}
    for slot, (name, src, dst) in enumerate((("o", o_hbm, ov), ("r", r_hbm, rv), ("x", x_hbm, xv), ("w", w_hbm, wv), ("t", t_hbm, tv), ("m", m_hbm, mv))):
        loads[name] = pltpu.make_async_copy(src, dst, load_sems.at[slot])
        loads[name].start()

    barrier = pltpu.get_barrier_semaphore()

    def greet(peer):
        pl.semaphore_signal(barrier, inc=1, device_id=peer, device_id_type=MESH)

    expected = 0
    if inner:
        for peer in (core, zlo, to_x(1), to_x(-1)):
            greet(peer)
        expected += 4
    if outer:
        greet(to_y(1))
        greet(to_y(-1))

        @pl.when(jnp.logical_not(last))
        def _():
            greet(to_h(above))

        @pl.when(jnp.logical_not(first))
        def _():
            greet(to_h(below))

        expected += 2 + jnp.where(last, 0, 1) + jnp.where(first, 0, 1)

    net = Copies(send_sems, recv_sems)

    def ycut(block):
        return slice(block * ycols, (block + 1) * ycols)

    def y_own(k, block):
        return ov[at_y(k), :, ycut(block)] - rv[at_y(k), :, ycut(block)].astype(F32)

    def y_send(direction, block, j):
        step = 1 if direction == 0 else -1
        value = y_own(step * j, block)
        if j < hops(direction, block, YB):
            net.arrived(("ry", direction, block, j + 1))
            value = value + dec(ry[direction, block, j])
        sy[direction, block, j - 1] = enc(value)
        net.start(("ry", direction, block, j), sy.at[direction, block, j - 1], ry.at[direction, block, j - 1], to_y(step))

    y_order = ((0, 0), (1, 2), (0, 1), (1, 3), (0, 2), (1, 0), (0, 3), (1, 1))

    def y_first():
        for direction, block in y_order:
            y_send(direction, block, hops(direction, block, YB))

    def y_round(j):
        if outer:
            for direction, block in y_order:
                if j < hops(direction, block, YB):
                    y_send(direction, block, j)

    def y_final(block):
        for direction in (0, 1):
            net.arrived(("ry", direction, block, 1))
        at = ycut(block)
        ysum[:, at] = y_own(0, block) + (dec(ry[0, block, 0]) + dec(ry[1, block, 0]))
        net.make(("up", block), us.at[:, at], ub.at[:, at], to_h(above), guard=jnp.logical_not(last))
        slot = dv.at[y, :, at]
        for target in range(NH - 1):
            net.make(("down", block, target), slot, slot, to_h(target), recv_like=("down", block, 0) if target else None, guard=last)

        @pl.when(jnp.logical_not(first))
        def _():
            net.arrived(("up", block))
            ysum[:, at] = ysum[:, at] + dec(ub[:, at])

        @pl.when(jnp.logical_not(last))
        def _():
            us[:, at] = enc(ysum[:, at])
            net.begin(("up", block))

        @pl.when(last)
        def _():
            dv[y, :, at] = enc(ysum[:, at] / REPS)
            for target in range(NH - 1):
                net.begin(("down", block, target))

    tiles = [(start, cols // 2) for start in (0, cols // 2)] + [(cols, toks)]

    def partial(core_index, ks, out, dtype):
        rows = jnp.concatenate([xv[at_x(k), :, core_index].reshape(NZ * 16, feats) for k in ks], axis=0)
        for start, width in tiles:
            right = wb[:, start:start + width] if start < cols else xt[...]
            value = jnp.dot(rows, right, preferred_element_type=F32).astype(dtype)
            for n, k in enumerate(ks):
                out[at_x(k), :, :, start:start + width] = value[n * NZ * 16:(n + 1) * NZ * 16].reshape(NZ, 16, width)

    merged = set()

    def merge(k):
        k = k % NX
        if k not in merged:
            merged.add(k)
            net.arrived(("core", k))
            qown[at_x(k)] = qown[at_x(k)] + qpar[at_x(k)].astype(F32)

    xcols = wide // XH

    def xcut(block):
        return slice((block % XH) * xcols, (block % XH + 1) * xcols)

    def zz(block):
        return 1 - z if block < XH else z

    def x_send(direction, block, j):
        step = 1 if direction == 0 else -1
        merge(step * j)
        value = qown[at_x(step * j), zz(block), :, xcut(block)]
        if j < hops(direction, block, XB):
            net.arrived(("rx", direction, block, j + 1))
            value = value + rx[direction, block, j].astype(F32)
        sx[direction, block, j - 1] = value.astype(BF16)
        net.start(("rx", direction, block, j), sx.at[direction, block, j - 1], rx.at[direction, block, j - 1], to_x(step))

    def x_final(net, block):
        for direction in (0, 1):
            net.arrived(("rx", direction, block, 1))
        return qown[x, zz(block), :, xcut(block)] + (rx[0, block, 0].astype(F32) + rx[1, block, 0].astype(F32))

    def halves(first_block, other_block):
        return [((0, first_block + n), (1, other_block + n)) for n in range(XH)]

    x_long = [pair for pairs in halves(0, XH) for pair in pairs]
    x_short = [pair for pairs in halves(XH, 0) for pair in pairs]
    x_order = x_long + x_short

    def x_round(j):
        if inner:
            for direction, block in x_order:
                if j < hops(direction, block, XB):
                    x_send(direction, block, j)

    def g_slot(k, block):
        return ek.at[at_x(k), z if block < XH else 1 - z, c, :, xcut(block)]

    def rest(net, late):
        def g_pass(direction, block, i):
            step = 1 if direction == 0 else -1
            slot = g_slot(-step * i, block)
            if i > 0:
                net.arrived(("gx", direction, block, i))
            if i < hops(direction, block, XB):
                net.start(("gx", direction, block, i + 1), slot, slot, to_x(step))
            if i > 0:
                net.start(("gc", direction, block, i), slot, slot, core)

        def g_own(block):
            for direction in (0, 1):
                g_pass(direction, block, 0)
            net.start(("gc", block), g_slot(0, block), g_slot(0, block), core)

        def g_hop(side, i):
            if inner:
                for block in range(side * XH, (side + 1) * XH):
                    for direction in (0, 1):
                        if i <= hops(direction, block, XB):
                            g_pass(direction, block, i)

        def d_pass(direction, block, i):
            step = 1 if direction == 0 else -1
            slot = dv.at[at_y(-step * i), :, ycut(block)]
            if i > 0:
                net.arrived(("gy", direction, block, i))
            if i < hops(direction, block, YB):
                net.start(("gy", direction, block, i + 1), slot, slot, to_y(step))

        def d_finish(k, block):
            at, row = ycut(block), at_y(k)
            delta = dec(dv[row, :, at])
            moment = momentum_coef * mv[row, :, at] + delta
            moved = ov[row, :, at] - outer_rate * (delta + momentum_coef * moment)
            m_out[row, :, at] = moment
            o_out[row, :, at] = moved
            r_out[row, :, at] = (merge_keep * rv[row, :, at].astype(F32) + (1.0 - merge_keep) * moved).astype(BF16)

        def d_own():
            if outer:
                for block in (0, 2, 1, 3):
                    @pl.when(jnp.logical_not(last))
                    def _():
                        net.arrived(("down", block, 0))

                    for direction in (0, 1):
                        d_pass(direction, block, 0)

        def d_own_finish():
            loads["m"].wait()
            if outer:
                for block in range(YB):
                    d_finish(0, block)

        def d_hop(i):
            if outer:
                pieces = [piece for piece in y_order if i <= hops(*piece, YB)]
                for direction, block in pieces:
                    d_pass(direction, block, i)
                for direction, block in pieces:
                    d_finish(-i if direction == 0 else i, block)

        def z_sends():
            if inner:
                for n in range(XH):
                    zs[:, xcut(n)] = x_final(net, n).astype(BF16)
                    net.start(("zr", n), zs.at[:, xcut(n)], zr.at[:, xcut(n)], zlo)

        def own_errors():
            if inner:
                loads["t"].wait()
                for n in range(XH):
                    mine = x_final(net, XH + n)
                    net.arrived(("zr", n))
                    total = mine + zr[:, xcut(n)].astype(F32)
                    low, high = n * xcols, (n + 1) * xcols
                    edge = min(max(cols, low), high)
                    if low < edge:
                        ek[x, z, c, :, low:edge] = (total[:, :edge - low] * weight_scale - tv[:, low:edge].astype(F32)).astype(BF16)
                    if edge < high:
                        ek[x, z, c, :, edge:high] = total[:, edge - low:].astype(BF16)
                    net.start(("gz", n), g_slot(0, n), g_slot(0, n), zlo)
                    g_own(n)

        def neighbour_errors():
            if inner:
                for n in range(XH):
                    net.arrived(("gz", n))
                    g_own(XH + n)

        def core_errors():
            if inner:
                for name in list(net.made):
                    if name[0] == "gc":
                        net.arrived(name)

        def last_product():
            if inner:
                turned = jnp.dot(xt[...], ek[:, :, :, :, cols:wide].reshape(toks, toks), preferred_element_type=F32)
                both = (2.0 * xt[...].astype(F32) - (inner_rate / D) * turned).astype(BF16)
                for start in range(0, cols, cols // 2):
                    at = slice(start, start + cols // 2)
                    gradient = jnp.dot(both, ek[:, :, :, :, at].reshape(toks, cols // 2), preferred_element_type=F32)
                    w_out[:, at] = wv[:, at] - (inner_rate * weight_scale) * gradient

        z_sends()
        if late:
            d_own()
            own_errors()
            d_own_finish()
            d_hop(1)
            g_hop(0, 1)
            neighbour_errors()
            d_hop(2)
            g_hop(0, 2)
            g_hop(1, 1)
            d_hop(3)
            g_hop(0, 3)
            g_hop(1, 2)
            d_hop(4)
            g_hop(0, 4)
            g_hop(1, 3)
            g_hop(1, 4)
            core_errors()
            last_product()
        else:
            own_errors()
            g_hop(0, 1)
            neighbour_errors()
            g_hop(0, 2)
            g_hop(1, 1)
            g_hop(0, 3)
            g_hop(1, 2)
            d_own()
            g_hop(0, 4)
            g_hop(1, 3)
            d_own_finish()
            d_hop(1)
            g_hop(1, 4)
            d_hop(2)
            core_errors()
            last_product()
            d_hop(3)
            d_hop(4)
        net.drain()

    if outer:
        loads["o"].wait()
        loads["r"].wait()
    pl.semaphore_wait(barrier, expected)
    if outer:
        y_first()
    loads["x"].wait()
    if inner:
        xt[...] = xv[...].reshape(toks, feats).T
    loads["w"].wait()
    if inner:
        wb[...] = wv[...].astype(BF16)
        for ks in ((4, 3), (5, 2), (6, 1), (7, 0)):
            partial(1 - c, ks, qoth, BF16)
            for k in ks:
                net.start(("core", k), qoth.at[at_x(k)], qpar.at[at_x(k)], core)
    y_round(3)
    if inner:
        partial(c, (4, 3, 5, 2, 6, 1, 7, 0), qown, F32)
        for direction, block in x_order:
            x_send(direction, block, hops(direction, block, XB))
    y_round(2)
    x_round(3)
    y_round(1)
    x_round(2)
    if outer:
        for block in (0, 2, 1, 3):
            y_final(block)
    x_round(1)
    if inner:
        merge(0)
    if not inner:
        loads["t"].wait()
    if not outer:
        loads["o"].wait()
        loads["r"].wait()

    @pl.when(h >= NH // 2)
    def _():
        rest(net.branch(), True)

    @pl.when(h < NH // 2)
    def _():
        rest(net.branch(), False)


def store_kernel(*refs):
    sems = refs[-1]
    half = (len(refs) - 1) // 2
    stores = [pltpu.make_async_copy(refs[n], refs[half + n], sems.at[n]) for n in range(half)]
    for store in stores:
        store.start()
    for store in stores:
        store.wait()


def store_results(results):
    return pl.pallas_call(
        store_kernel,
        out_shape=tuple(pltpu.HBM(result.shape, result.dtype) for result in results),
        in_specs=[pl.BlockSpec(memory_space=pl.ANY)] * len(results),
        out_specs=(pl.BlockSpec(memory_space=pltpu.HBM),) * len(results),
        scratch_shapes=[pltpu.SemaphoreType.DMA((len(results),))],
        compiler_params=pltpu.CompilerParams(vmem_limit_bytes=2 << 20),
    )(*results)


def exchange(tokens, targets, weights, outer_weights, moment, replica, inner=True, outer=True):
    toks, feats = tokens.shape
    cols = weights.shape[1]
    wide = cols + toks
    o_cols = outer_weights.shape[1]
    y_rows = outer_weights.shape[0] // NY
    weight_scale = D ** (-0.5)
    hbm = pl.BlockSpec(memory_space=pl.ANY)
    copies = 200
    results = pl.pallas_call(
        functools.partial(comm_kernel, inner, outer, weight_scale),
        out_shape=(
            jax.ShapeDtypeStruct((feats, cols), F32),
            jax.ShapeDtypeStruct((NY, y_rows, o_cols), F32),
            jax.ShapeDtypeStruct((NY, y_rows, o_cols), F32),
            jax.ShapeDtypeStruct((NY, y_rows, o_cols), BF16),
        ),
        in_specs=[hbm] * 6,
        out_specs=(pl.BlockSpec(memory_space=pltpu.VMEM),) * 4,
        scratch_shapes=[
            pltpu.VMEM((NX, NZ, NC, 16, feats), BF16),
            pltpu.VMEM((feats, toks), BF16),
            pltpu.VMEM((feats, cols), F32),
            pltpu.VMEM((feats, cols), BF16),
            pltpu.VMEM((16, cols), BF16),
            pltpu.VMEM((NY, y_rows, o_cols), F32),
            pltpu.VMEM((NY, y_rows, o_cols), BF16),
            pltpu.VMEM((NY, y_rows, o_cols), F32),
            pltpu.VMEM((NX, NZ, 16, wide), F32),
            pltpu.VMEM((NX, NZ, 16, wide), BF16),
            pltpu.VMEM((NX, NZ, 16, wide), BF16),
            pltpu.VMEM((2, XB, 4, 16, wide // XH), BF16),
            pltpu.VMEM((2, XB, 4, 16, wide // XH), BF16),
            pltpu.VMEM((16, wide), BF16),
            pltpu.VMEM((16, wide), BF16),
            pltpu.VMEM((NX, NZ, NC, 16, wide), BF16),
            pltpu.VMEM((2, YB, 4, y_rows, o_cols // YB), BF16),
            pltpu.VMEM((2, YB, 4, y_rows, o_cols // YB), BF16),
            pltpu.VMEM((y_rows, o_cols), F32),
            pltpu.VMEM((y_rows, o_cols), BF16),
            pltpu.VMEM((y_rows, o_cols), BF16),
            pltpu.VMEM((NY, y_rows, o_cols), BF16),
            pltpu.SemaphoreType.DMA((6,)),
            pltpu.SemaphoreType.DMA((copies,)),
            pltpu.SemaphoreType.DMA((copies,)),
        ],
        compiler_params=pltpu.CompilerParams(collective_id=0, has_side_effects=True, vmem_limit_bytes=32 << 20),
    )(
        *(pltpu.with_memory_space_constraint(array, pltpu.HBM) for array in (
            tokens.reshape(NX, NZ, NC, 16, feats),
            weights,
            targets,
            outer_weights.reshape(NY, y_rows, o_cols),
            replica.reshape(NY, y_rows, o_cols),
            moment.reshape(NY, y_rows, o_cols),
        ))
    )
    return results[0], *(result.reshape(outer_weights.shape) for result in results[1:])


def local(tokens, targets, inner_weights, outer_weights, outer_momentum, replica_weights):
    new_inner, new_outer, new_moment, merged = store_results(exchange(
        tokens[0], targets[0], inner_weights[0], outer_weights, outer_momentum, replica_weights[0]
    ))
    return (new_inner[None], new_outer, new_moment, merged[None])


def solution(mesh):
    placed = (
        P("rep", None, "fsdp"),
        P("rep", "fsdp", None),
        P("rep", "fsdp", None),
        P("fsdp", None),
        P("fsdp", None),
        P("rep", "fsdp", None),
    )
    return jax.shard_map(
        local,
        mesh=mesh,
        in_specs=placed,
        out_specs=(
            P("rep", "fsdp", None),
            P("fsdp", None),
            P("fsdp", None),
            P("rep", "fsdp", None),
        ),
        check_vma=False,
    )
```

```python
import functools

import jax
import jax.numpy as jnp
from jax import lax
from jax.experimental import pallas as pl
from jax.experimental.pallas import tpu as pltpu
from jax.sharding import PartitionSpec as P

D = 8192
REPS = 32
inner_rate = 0.5
momentum_coef = 0.9
outer_rate = 0.7
merge_keep = 0.5

NX, NZ, NC = 8, 2, 2
NY, NH = 8, 4
MESH = pl.DeviceIdType.MESH
F32, BF16 = jnp.float32, jnp.bfloat16


class Copies:
    def __init__(self, send_sems, recv_sems, slots=None, made=None):
        self.send_sems, self.recv_sems = send_sems, recv_sems
        self.slots = {} if slots is None else slots
        self.made = {} if made is None else dict(made)

    def branch(self):
        return Copies(self.send_sems, self.recv_sems, self.slots, self.made)

    def make(self, name, src, dst, device, recv_like=None, guard=None):
        slot = self.slots.setdefault(name, len(self.slots))
        assert slot < self.send_sems.shape[0]
        copy = pltpu.make_async_remote_copy(
            src_ref=src,
            dst_ref=dst,
            send_sem=self.send_sems.at[slot],
            recv_sem=self.recv_sems.at[slot if recv_like is None else self.slots[recv_like]],
            device_id=device,
            device_id_type=MESH,
        )
        self.made[name] = (copy, guard)
        return copy

    def start(self, name, src, dst, device):
        self.make(name, src, dst, device).start()

    def begin(self, name):
        self.made[name][0].start()

    def arrived(self, name):
        self.made[name][0].wait_recv()

    def drain(self):
        for copy, guard in self.made.values():
            if guard is None:
                copy.wait_send()
            else:
                pl.when(guard)(copy.wait_send)


def enc(value):
    return (value * jnp.abs(value) * (value * value)).astype(BF16)


def dec(coded):
    coded = coded.astype(F32)
    root = jnp.sqrt(jnp.sqrt(jnp.abs(coded)))
    return jnp.where(coded < 0.0, -root, root)


YB = 4
XH = 2
XB = 2 * XH


def hops(direction, block, blocks):
    return 4 if (direction == 0) == (block < blocks // 2) else 3


def comm_kernel(inner, outer, weight_scale, x_hbm, w_hbm, t_hbm, o_hbm, r_hbm, m_hbm,
                w_out, o_out, m_out, r_out,
                xv, xt, wv, wb, tv, ov, rv, mv, qown, qoth, qpar, rx, sx, zs, zr, ek,
                ry, sy, ysum, us, ub, dv,
                load_sems, send_sems, recv_sems):
    rep, fsdp = lax.axis_index("rep"), lax.axis_index("fsdp")
    x, z, c = fsdp // 4, (fsdp // 2) % 2, fsdp % 2
    y, h = rep // 4, rep % 4
    feats, cols = wv.shape
    toks = xt.shape[1]
    wide = cols + toks
    ycols = ov.shape[2] // YB

    def at_x(k):
        return lax.rem(x + k + NX, NX)

    def at_y(k):
        return lax.rem(y + k + NY, NY)

    def to_x(k):
        return {"fsdp": at_x(k) * 4 + z * 2 + c}

    def to_y(k):
        return {"rep": at_y(k) * 4 + h}

    def to_h(at):
        return {"rep": y * 4 + at}

    core = {"fsdp": x * 4 + z * 2 + 1 - c}
    zlo = {"fsdp": x * 4 + (1 - z) * 2 + c}
    above, below = lax.rem(h + 1, NH), lax.rem(h + NH - 1, NH)
    first, last = h == 0, h == NH - 1

    loads = {}
    for slot, (name, src, dst) in enumerate((("o", o_hbm, ov), ("r", r_hbm, rv), ("x", x_hbm, xv), ("w", w_hbm, wv), ("t", t_hbm, tv), ("m", m_hbm, mv))):
        loads[name] = pltpu.make_async_copy(src, dst, load_sems.at[slot])
        loads[name].start()

    barrier = pltpu.get_barrier_semaphore()

    def greet(peer):
        pl.semaphore_signal(barrier, inc=1, device_id=peer, device_id_type=MESH)

    expected = 0
    if inner:
        for peer in (core, zlo, to_x(1), to_x(-1)):
            greet(peer)
        expected += 4
    if outer:
        greet(to_y(1))
        greet(to_y(-1))

        @pl.when(jnp.logical_not(last))
        def _():
            greet(to_h(above))

        @pl.when(jnp.logical_not(first))
        def _():
            greet(to_h(below))

        expected += 2 + jnp.where(last, 0, 1) + jnp.where(first, 0, 1)

    net = Copies(send_sems, recv_sems)

    def ycut(block):
        return slice(block * ycols, (block + 1) * ycols)

    def y_own(k, block):
        return ov[at_y(k), :, ycut(block)] - rv[at_y(k), :, ycut(block)].astype(F32)

    def y_send(direction, block, j):
        step = 1 if direction == 0 else -1
        value = y_own(step * j, block)
        if j < hops(direction, block, YB):
            net.arrived(("ry", direction, block, j + 1))
            value = value + dec(ry[direction, block, j])
        sy[direction, block, j - 1] = enc(value)
        net.start(("ry", direction, block, j), sy.at[direction, block, j - 1], ry.at[direction, block, j - 1], to_y(step))

    y_order = ((0, 0), (1, 2), (0, 1), (1, 3), (0, 2), (1, 0), (0, 3), (1, 1))

    def y_first():
        for direction, block in y_order:
            y_send(direction, block, hops(direction, block, YB))

    def y_round(j):
        if outer:
            for direction, block in y_order:
                if j < hops(direction, block, YB):
                    y_send(direction, block, j)

    def y_final(block):
        for direction in (0, 1):
            net.arrived(("ry", direction, block, 1))
        at = ycut(block)
        ysum[:, at] = y_own(0, block) + (dec(ry[0, block, 0]) + dec(ry[1, block, 0]))
        net.make(("up", block), us.at[block], ub.at[block], to_h(above), guard=jnp.logical_not(last))
        slot = dv.at[y, block]
        for target in range(NH - 1):
            net.make(("down", block, target), slot, slot, to_h(target), recv_like=("down", block, 0) if target else None, guard=last)

        @pl.when(jnp.logical_not(first))
        def _():
            net.arrived(("up", block))
            ysum[:, at] = ysum[:, at] + dec(ub[block])

        @pl.when(jnp.logical_not(last))
        def _():
            us[block] = enc(ysum[:, at])
            net.begin(("up", block))

        @pl.when(last)
        def _():
            dv[y, block] = enc(ysum[:, at] / REPS)
            net.begin(("down", block, 0))

    def y_spread():
        @pl.when(last)
        def _():
            for target in range(1, NH - 1):
                for block in range(YB):
                    net.begin(("down", block, target))

    tiles = [(start, cols // 2) for start in (0, cols // 2)] + [(cols, toks)]

    def partial(core_index, ks, out, dtype):
        rows = jnp.concatenate([xv[at_x(k), :, core_index].reshape(NZ * 16, feats) for k in ks], axis=0)
        for start, width in tiles:
            right = wb[:, start:start + width] if start < cols else xt[...]
            value = jnp.dot(rows, right, preferred_element_type=F32).astype(dtype)
            for n, k in enumerate(ks):
                out[at_x(k), :, :, start:start + width] = value[n * NZ * 16:(n + 1) * NZ * 16].reshape(NZ, 16, width)

    merged = set()

    def merge(k):
        k = k % NX
        if k not in merged:
            merged.add(k)
            net.arrived(("core", k))
            qown[at_x(k)] = qown[at_x(k)] + qpar[at_x(k)].astype(F32)

    xcols = wide // XH

    def xcut(block):
        return slice((block % XH) * xcols, (block % XH + 1) * xcols)

    def zz(block):
        return 1 - z if block < XH else z

    def x_send(direction, block, j):
        step = 1 if direction == 0 else -1
        merge(step * j)
        value = qown[at_x(step * j), zz(block), :, xcut(block)]
        if j < hops(direction, block, XB):
            net.arrived(("rx", direction, block, j + 1))
            value = value + rx[direction, block, j].astype(F32)
        sx[direction, block, j - 1] = value.astype(BF16)
        net.start(("rx", direction, block, j), sx.at[direction, block, j - 1], rx.at[direction, block, j - 1], to_x(step))

    def x_final(net, block):
        for direction in (0, 1):
            net.arrived(("rx", direction, block, 1))
        return qown[x, zz(block), :, xcut(block)] + (rx[0, block, 0].astype(F32) + rx[1, block, 0].astype(F32))

    def halves(first_block, other_block):
        return [((0, first_block + n), (1, other_block + n)) for n in range(XH)]

    x_long = [pair for pairs in halves(0, XH) for pair in pairs]
    x_short = [pair for pairs in halves(XH, 0) for pair in pairs]
    x_order = x_long + x_short

    def x_round(j):
        if inner:
            for direction, block in x_order:
                if j < hops(direction, block, XB):
                    x_send(direction, block, j)

    def g_slot(k, block):
        return ek.at[at_x(k), z if block < XH else 1 - z, c, :, xcut(block)]

    def rest(net, late):
        def g_pass(direction, block, i):
            step = 1 if direction == 0 else -1
            slot = g_slot(-step * i, block)
            if i > 0:
                net.arrived(("gx", direction, block, i))
            if i < hops(direction, block, XB):
                net.start(("gx", direction, block, i + 1), slot, slot, to_x(step))
            if i > 0:
                net.start(("gc", direction, block, i), slot, slot, core)

        def g_own(block):
            for direction in (0, 1):
                g_pass(direction, block, 0)
            net.start(("gc", block), g_slot(0, block), g_slot(0, block), core)

        def g_hop(side, i):
            if inner:
                for block in range(side * XH, (side + 1) * XH):
                    for direction in (0, 1):
                        if i <= hops(direction, block, XB):
                            g_pass(direction, block, i)

        def d_pass(direction, block, i):
            step = 1 if direction == 0 else -1
            slot = dv.at[at_y(-step * i), block]
            if i > 0:
                net.arrived(("gy", direction, block, i))
            if i < hops(direction, block, YB):
                net.start(("gy", direction, block, i + 1), slot, slot, to_y(step))

        def d_finish(k, block):
            at, row = ycut(block), at_y(k)
            delta = dec(dv[row, block])
            moment = momentum_coef * mv[row, :, at] + delta
            moved = ov[row, :, at] - outer_rate * (delta + momentum_coef * moment)
            m_out[row, :, at] = moment
            o_out[row, :, at] = moved
            r_out[row, :, at] = (merge_keep * rv[row, :, at].astype(F32) + (1.0 - merge_keep) * moved).astype(BF16)

        def d_own():
            if outer:
                for block in (0, 2, 1, 3):
                    @pl.when(jnp.logical_not(last))
                    def _():
                        net.arrived(("down", block, 0))

                    for direction in (0, 1):
                        d_pass(direction, block, 0)

        def d_own_finish():
            loads["m"].wait()
            if outer:
                for block in range(YB):
                    d_finish(0, block)

        def d_hop(i):
            if outer:
                pieces = [piece for piece in y_order if i <= hops(*piece, YB)]
                for direction, block in pieces:
                    d_pass(direction, block, i)
                for direction, block in pieces:
                    d_finish(-i if direction == 0 else i, block)

        def z_sends():
            if inner:
                for n in range(XH):
                    zs[:, xcut(n)] = x_final(net, n).astype(BF16)
                    net.start(("zr", n), zs.at[:, xcut(n)], zr.at[:, xcut(n)], zlo)

        def own_errors():
            if inner:
                loads["t"].wait()
                for n in range(XH):
                    mine = x_final(net, XH + n)
                    net.arrived(("zr", n))
                    total = mine + zr[:, xcut(n)].astype(F32)
                    low, high = n * xcols, (n + 1) * xcols
                    edge = min(max(cols, low), high)
                    if low < edge:
                        ek[x, z, c, :, low:edge] = (total[:, :edge - low] * weight_scale - tv[:, low:edge].astype(F32)).astype(BF16)
                    if edge < high:
                        ek[x, z, c, :, edge:high] = total[:, edge - low:].astype(BF16)
                    net.start(("gz", n), g_slot(0, n), g_slot(0, n), zlo)
                    g_own(n)

        def neighbour_errors():
            if inner:
                for n in range(XH):
                    net.arrived(("gz", n))
                    g_own(XH + n)

        def core_errors():
            if inner:
                for name in list(net.made):
                    if name[0] == "gc":
                        net.arrived(name)

        def last_product():
            if inner:
                turned = jnp.dot(xt[...], ek[:, :, :, :, cols:wide].reshape(toks, toks), preferred_element_type=F32)
                both = (2.0 * xt[...].astype(F32) - (inner_rate / D) * turned).astype(BF16)
                for start in range(0, cols, cols // 2):
                    at = slice(start, start + cols // 2)
                    gradient = jnp.dot(both, ek[:, :, :, :, at].reshape(toks, cols // 2), preferred_element_type=F32)
                    w_out[:, at] = wv[:, at] - (inner_rate * weight_scale) * gradient

        z_sends()
        if late:
            d_own()
            own_errors()
            d_own_finish()
            d_hop(1)
            g_hop(0, 1)
            neighbour_errors()
            d_hop(2)
            g_hop(0, 2)
            g_hop(1, 1)
            d_hop(3)
            g_hop(0, 3)
            g_hop(1, 2)
            d_hop(4)
            g_hop(0, 4)
            g_hop(1, 3)
            g_hop(1, 4)
            core_errors()
            last_product()
        else:
            own_errors()
            g_hop(0, 1)
            neighbour_errors()
            g_hop(0, 2)
            g_hop(1, 1)
            g_hop(0, 3)
            g_hop(1, 2)
            d_own()
            d_own_finish()
            d_hop(1)
            g_hop(0, 4)
            g_hop(1, 3)
            d_hop(2)
            g_hop(1, 4)
            d_hop(3)
            core_errors()
            last_product()
            d_hop(4)
        net.drain()

    if outer:
        loads["o"].wait()
        loads["r"].wait()
    pl.semaphore_wait(barrier, expected)
    if outer:
        y_first()
    loads["x"].wait()
    if inner:
        xt[...] = xv[...].reshape(toks, feats).T
    loads["w"].wait()
    if inner:
        wb[...] = wv[...].astype(BF16)
        for ks in ((4, 3), (5, 2), (6, 1), (7, 0)):
            partial(1 - c, ks, qoth, BF16)
            for k in ks:
                net.start(("core", k), qoth.at[at_x(k)], qpar.at[at_x(k)], core)
    y_round(3)
    if inner:
        partial(c, (4, 3, 5, 2, 6, 1, 7, 0), qown, F32)
    y_round(2)
    if inner:
        for direction, block in x_order:
            x_send(direction, block, hops(direction, block, XB))
    y_round(1)
    x_round(3)
    if outer:
        for block in (0, 2, 1, 3):
            y_final(block)
        y_spread()
    x_round(2)
    x_round(1)
    if inner:
        merge(0)
    if not inner:
        loads["t"].wait()
    if not outer:
        loads["o"].wait()
        loads["r"].wait()

    @pl.when(h >= NH // 2)
    def _():
        rest(net.branch(), True)

    @pl.when(h < NH // 2)
    def _():
        rest(net.branch(), False)


def store_kernel(*refs):
    sems = refs[-1]
    half = (len(refs) - 1) // 2
    stores = [pltpu.make_async_copy(refs[n], refs[half + n], sems.at[n]) for n in range(half)]
    for store in stores:
        store.start()
    for store in stores:
        store.wait()


def store_results(results):
    return pl.pallas_call(
        store_kernel,
        out_shape=tuple(pltpu.HBM(result.shape, result.dtype) for result in results),
        in_specs=[pl.BlockSpec(memory_space=pl.ANY)] * len(results),
        out_specs=(pl.BlockSpec(memory_space=pltpu.HBM),) * len(results),
        scratch_shapes=[pltpu.SemaphoreType.DMA((len(results),))],
        compiler_params=pltpu.CompilerParams(vmem_limit_bytes=2 << 20),
    )(*results)


def exchange(tokens, targets, weights, outer_weights, moment, replica, inner=True, outer=True):
    toks, feats = tokens.shape
    cols = weights.shape[1]
    wide = cols + toks
    o_cols = outer_weights.shape[1]
    y_rows = outer_weights.shape[0] // NY
    weight_scale = D ** (-0.5)
    hbm = pl.BlockSpec(memory_space=pl.ANY)
    copies = 200
    results = pl.pallas_call(
        functools.partial(comm_kernel, inner, outer, weight_scale),
        out_shape=(
            jax.ShapeDtypeStruct((feats, cols), F32),
            jax.ShapeDtypeStruct((NY, y_rows, o_cols), F32),
            jax.ShapeDtypeStruct((NY, y_rows, o_cols), F32),
            jax.ShapeDtypeStruct((NY, y_rows, o_cols), BF16),
        ),
        in_specs=[hbm] * 6,
        out_specs=(pl.BlockSpec(memory_space=pltpu.VMEM),) * 4,
        scratch_shapes=[
            pltpu.VMEM((NX, NZ, NC, 16, feats), BF16),
            pltpu.VMEM((feats, toks), BF16),
            pltpu.VMEM((feats, cols), F32),
            pltpu.VMEM((feats, cols), BF16),
            pltpu.VMEM((16, cols), BF16),
            pltpu.VMEM((NY, y_rows, o_cols), F32),
            pltpu.VMEM((NY, y_rows, o_cols), BF16),
            pltpu.VMEM((NY, y_rows, o_cols), F32),
            pltpu.VMEM((NX, NZ, 16, wide), F32),
            pltpu.VMEM((NX, NZ, 16, wide), BF16),
            pltpu.VMEM((NX, NZ, 16, wide), BF16),
            pltpu.VMEM((2, XB, 4, 16, wide // XH), BF16),
            pltpu.VMEM((2, XB, 4, 16, wide // XH), BF16),
            pltpu.VMEM((16, wide), BF16),
            pltpu.VMEM((16, wide), BF16),
            pltpu.VMEM((NX, NZ, NC, 16, wide), BF16),
            pltpu.VMEM((2, YB, 4, y_rows, o_cols // YB), BF16),
            pltpu.VMEM((2, YB, 4, y_rows, o_cols // YB), BF16),
            pltpu.VMEM((y_rows, o_cols), F32),
            pltpu.VMEM((YB, y_rows, o_cols // YB), BF16),
            pltpu.VMEM((YB, y_rows, o_cols // YB), BF16),
            pltpu.VMEM((NY, YB, y_rows, o_cols // YB), BF16),
            pltpu.SemaphoreType.DMA((6,)),
            pltpu.SemaphoreType.DMA((copies,)),
            pltpu.SemaphoreType.DMA((copies,)),
        ],
        compiler_params=pltpu.CompilerParams(collective_id=0, has_side_effects=True, vmem_limit_bytes=32 << 20),
    )(
        *(pltpu.with_memory_space_constraint(array, pltpu.HBM) for array in (
            tokens.reshape(NX, NZ, NC, 16, feats),
            weights,
            targets,
            outer_weights.reshape(NY, y_rows, o_cols),
            replica.reshape(NY, y_rows, o_cols),
            moment.reshape(NY, y_rows, o_cols),
        ))
    )
    return results[0], *(result.reshape(outer_weights.shape) for result in results[1:])


def local(tokens, targets, inner_weights, outer_weights, outer_momentum, replica_weights):
    new_inner, new_outer, new_moment, merged = store_results(exchange(
        tokens[0], targets[0], inner_weights[0], outer_weights, outer_momentum, replica_weights[0]
    ))
    return (new_inner[None], new_outer, new_moment, merged[None])


def solution(mesh):
    placed = (
        P("rep", None, "fsdp"),
        P("rep", "fsdp", None),
        P("rep", "fsdp", None),
        P("fsdp", None),
        P("fsdp", None),
        P("rep", "fsdp", None),
    )
    return jax.shard_map(
        local,
        mesh=mesh,
        in_specs=placed,
        out_specs=(
            P("rep", "fsdp", None),
            P("fsdp", None),
            P("fsdp", None),
            P("rep", "fsdp", None),
        ),
        check_vma=False,
    )
```

```python
import functools

import jax
import jax.numpy as jnp
from jax import lax
from jax.experimental import pallas as pl
from jax.experimental.pallas import tpu as pltpu
from jax.sharding import PartitionSpec as P

D = 8192
REPS = 32
inner_rate = 0.5
momentum_coef = 0.9
outer_rate = 0.7
merge_keep = 0.5

NX, NZ, NC = 8, 2, 2
NY, NH = 8, 4
MESH = pl.DeviceIdType.MESH
F32, BF16 = jnp.float32, jnp.bfloat16


class Copies:
    def __init__(self, send_sems, recv_sems, slots=None, made=None):
        self.send_sems, self.recv_sems = send_sems, recv_sems
        self.slots = {} if slots is None else slots
        self.made = {} if made is None else dict(made)

    def branch(self):
        return Copies(self.send_sems, self.recv_sems, self.slots, self.made)

    def make(self, name, src, dst, device, recv_like=None, guard=None):
        slot = self.slots.setdefault(name, len(self.slots))
        assert slot < self.send_sems.shape[0]
        copy = pltpu.make_async_remote_copy(
            src_ref=src,
            dst_ref=dst,
            send_sem=self.send_sems.at[slot],
            recv_sem=self.recv_sems.at[slot if recv_like is None else self.slots[recv_like]],
            device_id=device,
            device_id_type=MESH,
        )
        self.made[name] = (copy, guard)
        return copy

    def start(self, name, src, dst, device):
        self.make(name, src, dst, device).start()

    def begin(self, name):
        self.made[name][0].start()

    def arrived(self, name):
        self.made[name][0].wait_recv()

    def drain(self):
        for copy, guard in self.made.values():
            if guard is None:
                copy.wait_send()
            else:
                pl.when(guard)(copy.wait_send)


def enc(value):
    return (value * jnp.abs(value) * (value * value)).astype(BF16)


def dec(coded):
    coded = coded.astype(F32)
    root = jnp.sqrt(jnp.sqrt(jnp.abs(coded)))
    return jnp.where(coded < 0.0, -root, root)


YB = 4
XH = 2
XB = 2 * XH


def hops(direction, block, blocks):
    return 4 if (direction == 0) == (block < blocks // 2) else 3


def comm_kernel(inner, outer, weight_scale, x_hbm, w_hbm, t_hbm, o_hbm, r_hbm, m_hbm,
                w_out, o_out, m_out, r_out,
                xv, xt, wv, wb, tv, ov, rv, mv, qown, qoth, qpar, rx, sx, zs, zr, ek,
                ry, sy, ysum, us, ub, dv,
                load_sems, send_sems, recv_sems):
    rep, fsdp = lax.axis_index("rep"), lax.axis_index("fsdp")
    x, z, c = fsdp // 4, (fsdp // 2) % 2, fsdp % 2
    y, h = rep // 4, rep % 4
    feats, cols = wv.shape
    toks = xt.shape[1]
    wide = cols + toks
    ycols = ov.shape[2] // YB

    def at_x(k):
        return lax.rem(x + k + NX, NX)

    def at_y(k):
        return lax.rem(y + k + NY, NY)

    def to_x(k):
        return {"fsdp": at_x(k) * 4 + z * 2 + c}

    def to_y(k):
        return {"rep": at_y(k) * 4 + h}

    def to_h(at):
        return {"rep": y * 4 + at}

    core = {"fsdp": x * 4 + z * 2 + 1 - c}
    zlo = {"fsdp": x * 4 + (1 - z) * 2 + c}
    above, below = lax.rem(h + 1, NH), lax.rem(h + NH - 1, NH)
    first, last = h == 0, h == NH - 1

    loads = {}
    for slot, (name, src, dst) in enumerate((("o", o_hbm, ov), ("r", r_hbm, rv), ("x", x_hbm, xv), ("w", w_hbm, wv), ("t", t_hbm, tv), ("m", m_hbm, mv))):
        loads[name] = pltpu.make_async_copy(src, dst, load_sems.at[slot])
        loads[name].start()

    barrier = pltpu.get_barrier_semaphore()

    def greet(peer):
        pl.semaphore_signal(barrier, inc=1, device_id=peer, device_id_type=MESH)

    expected = 0
    if inner:
        for peer in (core, zlo, to_x(1), to_x(-1)):
            greet(peer)
        expected += 4
    if outer:
        greet(to_y(1))
        greet(to_y(-1))

        @pl.when(jnp.logical_not(last))
        def _():
            greet(to_h(above))

        @pl.when(jnp.logical_not(first))
        def _():
            greet(to_h(below))

        expected += 2 + jnp.where(last, 0, 1) + jnp.where(first, 0, 1)

    net = Copies(send_sems, recv_sems)

    def ycut(block):
        return slice(block * ycols, (block + 1) * ycols)

    def y_own(k, block):
        return ov[at_y(k), :, ycut(block)] - rv[at_y(k), :, ycut(block)].astype(F32)

    def y_send(net, direction, block, j):
        step = 1 if direction == 0 else -1
        value = y_own(step * j, block)
        if j < hops(direction, block, YB):
            net.arrived(("ry", direction, block, j + 1))
            value = value + dec(ry[direction, block, j])
        sy[direction, block, j - 1] = enc(value)
        net.start(("ry", direction, block, j), sy.at[direction, block, j - 1], ry.at[direction, block, j - 1], to_y(step))

    y_order = ((0, 0), (1, 2), (0, 1), (1, 3), (0, 2), (1, 0), (0, 3), (1, 1))

    def y_first():
        for direction, block in y_order:
            y_send(net, direction, block, hops(direction, block, YB))

    tiles = [(start, cols // 2) for start in (0, cols // 2)] + [(cols, toks)]

    def partial(core_index, ks, out, dtype):
        rows = jnp.concatenate([xv[at_x(k), :, core_index].reshape(NZ * 16, feats) for k in ks], axis=0)
        for start, width in tiles:
            right = wb[:, start:start + width] if start < cols else xt[...]
            value = jnp.dot(rows, right, preferred_element_type=F32).astype(dtype)
            for n, k in enumerate(ks):
                out[at_x(k), :, :, start:start + width] = value[n * NZ * 16:(n + 1) * NZ * 16].reshape(NZ, 16, width)

    def rest(net, late):
        merged = set()

        def y_round(j):
            if outer:
                for direction, block in y_order:
                    if j < hops(direction, block, YB):
                        y_send(net, direction, block, j)

        def y_final(block):
            for direction in (0, 1):
                net.arrived(("ry", direction, block, 1))
            at = ycut(block)
            ysum[:, at] = y_own(0, block) + (dec(ry[0, block, 0]) + dec(ry[1, block, 0]))
            net.make(("up", block), us.at[block], ub.at[block], to_h(above), guard=jnp.logical_not(last))
            slot = dv.at[y, block]
            for target in range(NH - 1):
                net.make(("down", block, target), slot, slot, to_h(target), recv_like=("down", block, 0) if target else None, guard=last)

            @pl.when(jnp.logical_not(first))
            def _():
                net.arrived(("up", block))
                ysum[:, at] = ysum[:, at] + dec(ub[block])

            @pl.when(jnp.logical_not(last))
            def _():
                us[block] = enc(ysum[:, at])
                net.begin(("up", block))

            @pl.when(last)
            def _():
                dv[y, block] = enc(ysum[:, at] / REPS)
                net.begin(("down", block, 0))

        def y_spread():
            @pl.when(last)
            def _():
                for target in range(1, NH - 1):
                    for block in range(YB):
                        net.begin(("down", block, target))

        def merge(k):
            k = k % NX
            if k not in merged:
                merged.add(k)
                net.arrived(("core", k))
                qown[at_x(k)] = qown[at_x(k)] + qpar[at_x(k)].astype(F32)

        xcols = wide // XH

        def xcut(block):
            return slice((block % XH) * xcols, (block % XH + 1) * xcols)

        def zz(block):
            return 1 - z if block < XH else z

        def x_send(direction, block, j):
            step = 1 if direction == 0 else -1
            merge(step * j)
            value = qown[at_x(step * j), zz(block), :, xcut(block)]
            if j < hops(direction, block, XB):
                net.arrived(("rx", direction, block, j + 1))
                value = value + rx[direction, block, j].astype(F32)
            sx[direction, block, j - 1] = value.astype(BF16)
            net.start(("rx", direction, block, j), sx.at[direction, block, j - 1], rx.at[direction, block, j - 1], to_x(step))

        def x_final(net, block):
            for direction in (0, 1):
                net.arrived(("rx", direction, block, 1))
            return qown[x, zz(block), :, xcut(block)] + (rx[0, block, 0].astype(F32) + rx[1, block, 0].astype(F32))

        def halves(first_block, other_block):
            return [((0, first_block + n), (1, other_block + n)) for n in range(XH)]

        x_long = [pair for pairs in halves(0, XH) for pair in pairs]
        x_short = [pair for pairs in halves(XH, 0) for pair in pairs]
        x_order = x_long + x_short

        def x_round(j):
            if inner:
                for direction, block in x_order:
                    if j < hops(direction, block, XB):
                        x_send(direction, block, j)

        def g_slot(k, block):
            return ek.at[at_x(k), z if block < XH else 1 - z, c, :, xcut(block)]

        def g_pass(direction, block, i):
            step = 1 if direction == 0 else -1
            slot = g_slot(-step * i, block)
            if i > 0:
                net.arrived(("gx", direction, block, i))
            if i < hops(direction, block, XB):
                net.start(("gx", direction, block, i + 1), slot, slot, to_x(step))
            if i > 0:
                net.start(("gc", direction, block, i), slot, slot, core)

        def g_own(block):
            for direction in (0, 1):
                g_pass(direction, block, 0)
            net.start(("gc", block), g_slot(0, block), g_slot(0, block), core)

        def g_hop(side, i):
            if inner:
                for block in range(side * XH, (side + 1) * XH):
                    for direction in (0, 1):
                        if i <= hops(direction, block, XB):
                            g_pass(direction, block, i)

        def d_pass(direction, block, i):
            step = 1 if direction == 0 else -1
            slot = dv.at[at_y(-step * i), block]
            if i > 0:
                net.arrived(("gy", direction, block, i))
            if i < hops(direction, block, YB):
                net.start(("gy", direction, block, i + 1), slot, slot, to_y(step))

        def d_finish(k, block):
            at, row = ycut(block), at_y(k)
            delta = dec(dv[row, block])
            moment = momentum_coef * mv[row, :, at] + delta
            moved = ov[row, :, at] - outer_rate * (delta + momentum_coef * moment)
            m_out[row, :, at] = moment
            o_out[row, :, at] = moved
            r_out[row, :, at] = (merge_keep * rv[row, :, at].astype(F32) + (1.0 - merge_keep) * moved).astype(BF16)

        def d_own():
            if outer:
                for block in (0, 2, 1, 3):
                    @pl.when(jnp.logical_not(last))
                    def _():
                        net.arrived(("down", block, 0))

                    for direction in (0, 1):
                        d_pass(direction, block, 0)

        def d_own_finish():
            loads["m"].wait()
            if outer:
                for block in range(YB):
                    d_finish(0, block)

        def d_hop(i):
            if outer:
                pieces = [piece for piece in y_order if i <= hops(*piece, YB)]
                for direction, block in pieces:
                    d_pass(direction, block, i)
                for direction, block in pieces:
                    d_finish(-i if direction == 0 else i, block)

        def z_sends():
            if inner:
                for n in range(XH):
                    zs[:, xcut(n)] = x_final(net, n).astype(BF16)
                    net.start(("zr", n), zs.at[:, xcut(n)], zr.at[:, xcut(n)], zlo)

        def own_errors():
            if inner:
                loads["t"].wait()
                for n in range(XH):
                    mine = x_final(net, XH + n)
                    net.arrived(("zr", n))
                    total = mine + zr[:, xcut(n)].astype(F32)
                    low, high = n * xcols, (n + 1) * xcols
                    edge = min(max(cols, low), high)
                    if low < edge:
                        ek[x, z, c, :, low:edge] = (total[:, :edge - low] * weight_scale - tv[:, low:edge].astype(F32)).astype(BF16)
                    if edge < high:
                        ek[x, z, c, :, edge:high] = total[:, edge - low:].astype(BF16)
                    net.start(("gz", n), g_slot(0, n), g_slot(0, n), zlo)
                    g_own(n)

        def neighbour_errors():
            if inner:
                for n in range(XH):
                    net.arrived(("gz", n))
                    g_own(XH + n)

        def core_errors():
            if inner:
                for name in list(net.made):
                    if name[0] == "gc":
                        net.arrived(name)

        def last_product():
            if inner:
                turned = jnp.dot(xt[...], ek[:, :, :, :, cols:wide].reshape(toks, toks), preferred_element_type=F32)
                both = (2.0 * xt[...].astype(F32) - (inner_rate / D) * turned).astype(BF16)
                for start in range(0, cols, cols // 2):
                    at = slice(start, start + cols // 2)
                    gradient = jnp.dot(both, ek[:, :, :, :, at].reshape(toks, cols // 2), preferred_element_type=F32)
                    w_out[:, at] = wv[:, at] - (inner_rate * weight_scale) * gradient

        def x_first():
            if inner:
                for direction, block in x_order:
                    x_send(direction, block, hops(direction, block, XB))

        def y_finals():
            if outer:
                for block in (0, 2, 1, 3):
                    y_final(block)
                y_spread()

        if late:
            y_round(3)
            y_round(2)
            x_first()
            y_round(1)
            x_round(3)
            y_finals()
            x_round(2)
            x_round(1)
        else:
            x_first()
            y_round(3)
            x_round(3)
            y_round(2)
            x_round(2)
            y_round(1)
            x_round(1)
        if inner:
            merge(0)
        z_sends()
        if not late:
            y_finals()
        if late:
            d_own()
            own_errors()
            d_own_finish()
            d_hop(1)
            g_hop(0, 1)
            neighbour_errors()
            d_hop(2)
            g_hop(0, 2)
            g_hop(1, 1)
            d_hop(3)
            g_hop(0, 3)
            g_hop(1, 2)
            d_hop(4)
            g_hop(0, 4)
            g_hop(1, 3)
            g_hop(1, 4)
            core_errors()
            last_product()
        else:
            own_errors()
            g_hop(0, 1)
            neighbour_errors()
            g_hop(0, 2)
            g_hop(1, 1)
            g_hop(0, 3)
            g_hop(1, 2)
            d_own()
            d_own_finish()
            d_hop(1)
            g_hop(0, 4)
            g_hop(1, 3)
            d_hop(2)
            g_hop(1, 4)
            d_hop(3)
            core_errors()
            last_product()
            d_hop(4)
        net.drain()

    if outer:
        loads["o"].wait()
        loads["r"].wait()
    pl.semaphore_wait(barrier, expected)
    if outer:
        y_first()
    loads["x"].wait()
    if inner:
        xt[...] = xv[...].reshape(toks, feats).T
    loads["w"].wait()
    if inner:
        wb[...] = wv[...].astype(BF16)
        for ks in ((4, 3), (5, 2), (6, 1), (7, 0)):
            partial(1 - c, ks, qoth, BF16)
            for k in ks:
                net.start(("core", k), qoth.at[at_x(k)], qpar.at[at_x(k)], core)
    if inner:
        partial(c, (4, 3, 5, 2, 6, 1, 7, 0), qown, F32)
    if not inner:
        loads["t"].wait()
    if not outer:
        loads["o"].wait()
        loads["r"].wait()

    @pl.when(h >= NH // 2)
    def _():
        rest(net.branch(), True)

    @pl.when(h < NH // 2)
    def _():
        rest(net.branch(), False)


def store_kernel(*refs):
    sems = refs[-1]
    half = (len(refs) - 1) // 2
    stores = [pltpu.make_async_copy(refs[n], refs[half + n], sems.at[n]) for n in range(half)]
    for store in stores:
        store.start()
    for store in stores:
        store.wait()


def store_results(results):
    return pl.pallas_call(
        store_kernel,
        out_shape=tuple(pltpu.HBM(result.shape, result.dtype) for result in results),
        in_specs=[pl.BlockSpec(memory_space=pl.ANY)] * len(results),
        out_specs=(pl.BlockSpec(memory_space=pltpu.HBM),) * len(results),
        scratch_shapes=[pltpu.SemaphoreType.DMA((len(results),))],
        compiler_params=pltpu.CompilerParams(vmem_limit_bytes=2 << 20),
    )(*results)


def exchange(tokens, targets, weights, outer_weights, moment, replica, inner=True, outer=True):
    toks, feats = tokens.shape
    cols = weights.shape[1]
    wide = cols + toks
    o_cols = outer_weights.shape[1]
    y_rows = outer_weights.shape[0] // NY
    weight_scale = D ** (-0.5)
    hbm = pl.BlockSpec(memory_space=pl.ANY)
    copies = 200
    results = pl.pallas_call(
        functools.partial(comm_kernel, inner, outer, weight_scale),
        out_shape=(
            jax.ShapeDtypeStruct((feats, cols), F32),
            jax.ShapeDtypeStruct((NY, y_rows, o_cols), F32),
            jax.ShapeDtypeStruct((NY, y_rows, o_cols), F32),
            jax.ShapeDtypeStruct((NY, y_rows, o_cols), BF16),
        ),
        in_specs=[hbm] * 6,
        out_specs=(pl.BlockSpec(memory_space=pltpu.VMEM),) * 4,
        scratch_shapes=[
            pltpu.VMEM((NX, NZ, NC, 16, feats), BF16),
            pltpu.VMEM((feats, toks), BF16),
            pltpu.VMEM((feats, cols), F32),
            pltpu.VMEM((feats, cols), BF16),
            pltpu.VMEM((16, cols), BF16),
            pltpu.VMEM((NY, y_rows, o_cols), F32),
            pltpu.VMEM((NY, y_rows, o_cols), BF16),
            pltpu.VMEM((NY, y_rows, o_cols), F32),
            pltpu.VMEM((NX, NZ, 16, wide), F32),
            pltpu.VMEM((NX, NZ, 16, wide), BF16),
            pltpu.VMEM((NX, NZ, 16, wide), BF16),
            pltpu.VMEM((2, XB, 4, 16, wide // XH), BF16),
            pltpu.VMEM((2, XB, 4, 16, wide // XH), BF16),
            pltpu.VMEM((16, wide), BF16),
            pltpu.VMEM((16, wide), BF16),
            pltpu.VMEM((NX, NZ, NC, 16, wide), BF16),
            pltpu.VMEM((2, YB, 4, y_rows, o_cols // YB), BF16),
            pltpu.VMEM((2, YB, 4, y_rows, o_cols // YB), BF16),
            pltpu.VMEM((y_rows, o_cols), F32),
            pltpu.VMEM((YB, y_rows, o_cols // YB), BF16),
            pltpu.VMEM((YB, y_rows, o_cols // YB), BF16),
            pltpu.VMEM((NY, YB, y_rows, o_cols // YB), BF16),
            pltpu.SemaphoreType.DMA((6,)),
            pltpu.SemaphoreType.DMA((copies,)),
            pltpu.SemaphoreType.DMA((copies,)),
        ],
        compiler_params=pltpu.CompilerParams(collective_id=0, has_side_effects=True, vmem_limit_bytes=32 << 20),
    )(
        *(pltpu.with_memory_space_constraint(array, pltpu.HBM) for array in (
            tokens.reshape(NX, NZ, NC, 16, feats),
            weights,
            targets,
            outer_weights.reshape(NY, y_rows, o_cols),
            replica.reshape(NY, y_rows, o_cols),
            moment.reshape(NY, y_rows, o_cols),
        ))
    )
    return results[0], *(result.reshape(outer_weights.shape) for result in results[1:])


def local(tokens, targets, inner_weights, outer_weights, outer_momentum, replica_weights):
    new_inner, new_outer, new_moment, merged = store_results(exchange(
        tokens[0], targets[0], inner_weights[0], outer_weights, outer_momentum, replica_weights[0]
    ))
    return (new_inner[None], new_outer, new_moment, merged[None])


def solution(mesh):
    placed = (
        P("rep", None, "fsdp"),
        P("rep", "fsdp", None),
        P("rep", "fsdp", None),
        P("fsdp", None),
        P("fsdp", None),
        P("rep", "fsdp", None),
    )
    return jax.shard_map(
        local,
        mesh=mesh,
        in_specs=placed,
        out_specs=(
            P("rep", "fsdp", None),
            P("fsdp", None),
            P("fsdp", None),
            P("rep", "fsdp", None),
        ),
        check_vma=False,
    )
```
